32 devices in a mesh: req: 16 (over z, y, core), tp: 2 (over x).
Axes of the slice: x: 2, y: 2, z: 4, core: 2. Of those that a mesh axis runs over, the one named last changes fastest.
Arguments:
- attn_ctx: bfloat16 [1024, 4096], P('req', 'tp'), may hold values from -6 to 6
- o_weight: bfloat16 [4096, 2880], P('tp'), may hold values from -0.09375 to 0.09375
- o_bias: bfloat16 [2880], replicated, may hold values from -3 to 3
- residual: bfloat16 [1024, 2880], P(('req', 'tp')), may hold values from -6 to 6
- post_gain: bfloat16 [2880], replicated, may hold values from 0.5 to 1.5
- router_weight: bfloat16 [2880, 8], replicated, may hold values from -0.01953125 to 0.01953125
- router_bias: float32 [8], replicated, may hold values from -0.4 to 0.4
- routes: int32 [1024, 4], P('req'), may hold values from 0 to 7, all different within a row; in each aligned block of 32 rows (0 to 31, 32 to 63, ...) at most 32 rows name the same one
- gate_up_weight: bfloat16 [16, 2880, 2, 1440], P('req', None, None, 'tp'), may hold values from -0.25 to 0.25
- gate_up_bias: bfloat16 [16, 2, 1440], P('req', None, 'tp'), may hold values from -3 to 3
- down_weight: bfloat16 [16, 1440, 2880], P('req', 'tp'), may hold values from -0.0546875 to 0.0546875
- down_bias: bfloat16 [8, 2880], replicated, may hold values from -3 to 3
- next_gain: bfloat16 [2880], replicated, may hold values from 0.5 to 1.5
Outputs:
- hidden_state: bfloat16 [1024, 2880], P(('req', 'tp'))
- normed_out: bfloat16 [1024, 2880], P(('req', 'tp'))
The draws below stay inside these ranges and needn't reach their ends.
Inputs may be any that keep to these rules, and one draw needn't show every extreme that they name: `routes`: each row names 4 different experts. In each aligned block of 32 rows no expert is named by more than 32 rows, a bound that some block reaches.
All inputs are finite; a program needn't handle non-finite values.
Results may differ from the reference program's by a relative error of at most 0.017.
Values may be sent and summed in bfloat16 or wider, within the bound.
A program may use at most 128 MiB of HBM per device.

```python
import math
import jax
import jax.numpy as jnp
import numpy as np
from jax import lax

D = 2880
HEADS = 64
HEAD_DIM = 64
FF = 2880
TOP = 4
EXPERTS = 8
ROWS_DEV = 32
ROWS = 1024
CAP = 32
N_REQ = 16
N_TP = 2


def steps_of(key, dims, split, smallest, top_value):
    factor_of = 1.0
    for position, shards_of in split:
        heights = jax.random.uniform(jax.random.fold_in(jax.random.fold_in(key, 6), position), (shards_of,), jnp.float32, smallest / len(split), top_value / len(split))
        factor_of = factor_of * jnp.repeat(jnp.exp(heights), dims[position] // shards_of).reshape((-1,) + (1,) * (len(dims) - 1 - position))
    return factor_of


def shared_out(rng, own, number, rows, number_of, top, bound, lean):
    order = jax.random.permutation(rng, number_of)
    crowded, usual = shares(number_of, rows * top, bound, lean, True), shares(number_of, rows * top, bound, lean, False)
    places = jnp.arange(number_of)

    def named(tallies, offset_by):
        used = int((tallies > 0).sum())
        fixed = max(1, used // 4)
        moved = fixed + (places - fixed + offset_by * (used - fixed)) % max(1, number_of - fixed)
        return jnp.zeros((number_of,), jnp.int32).at[order[jnp.where(places < fixed, places, moved)]].set(jnp.asarray(tallies, jnp.int32))

    tallies = jnp.where(number % 4 == 0, named(crowded, number // 4), named(usual, number - number // 4 - 1))
    mixed = jax.random.permutation(jax.random.fold_in(own, 3), number_of)
    giver, sink = mixed[0:number_of // 2 * 2:2], mixed[1:number_of // 2 * 2:2]
    room = jnp.minimum(tallies[giver] - 1, bound - tallies[sink]) // 2
    room = jnp.where((giver == order[0]) | (sink == order[0]) | (tallies[sink] == 0), 0, jnp.maximum(room, 0))
    moved = jax.random.randint(jax.random.fold_in(own, 4), (number_of // 2,), 0, 1 << 20) % (room + 1)
    tallies = tallies.at[giver].add(-moved).at[sink].add(moved)
    labels = jnp.searchsorted(jnp.cumsum(tallies), jnp.arange(rows * top), side="right").astype(jnp.int32)
    grid = labels.reshape(top, rows).T
    grid = grid[jax.random.permutation(jax.random.fold_in(own, 1), rows)]
    offset_by = jax.random.randint(jax.random.fold_in(own, 2), (rows, 1), 0, top)
    return jnp.take_along_axis(grid, (jnp.arange(top)[None, :] + offset_by) % top, axis=1)


def shares(amount, total, bound, lean, full):
    loads = [(1 << 20) // math.isqrt(rank ** lean) + 1 for rank in range(1, amount + 1)]
    largest = bound if full else min(bound, max(-(-total // amount), total * loads[0] // sum(loads)))
    least = 1 if total - largest >= amount - 1 else 0
    counts, surplus = [largest] + [least] * (amount - 1), total - largest - least * (amount - 1)
    while surplus > 0:
        candidates = [i for i in range(1, amount) if counts[i] < largest] or [i for i in range(1, amount) if counts[i] < bound]
        mass, budget = sum([loads[i] for i in candidates]), surplus
        for i in candidates:
            more = min(bound - counts[i], max(1, budget * loads[i] // mass), surplus)
            counts[i] = counts[i] + more
            surplus = surplus - more
    return np.array(counts)


def noise(stream_key, extent, deviation, limit, shards=(), held_as=jnp.bfloat16):
    factor_of = steps_of(stream_key, extent, shards, -0.22, 0.18) if shards else 1.0
    drawn = jax.random.normal(stream_key, extent, jnp.float32) * deviation * factor_of
    return jnp.minimum(jnp.maximum(drawn, -limit), limit).astype(held_as)


def setup_inputs(seed: int = 0) -> dict:
    key_list = jax.random.split(jax.random.key(seed), 14)
    attn_ctx = noise(key_list[0], (ROWS, HEADS * HEAD_DIM), 1.0, 6.0, ((0, 16), (1, 2)))
    o_weight = noise(key_list[1], (HEADS * HEAD_DIM, D), (HEADS * HEAD_DIM) ** -0.5, 0.09375, ((0, 2),))
    o_bias = noise(key_list[2], (D,), 0.5, 3.0)
    residual = noise(key_list[3], (ROWS, D), 1.0, 6.0, ((0, 32),))
    post_gain = jnp.clip(1.0 + 0.1 * jax.random.normal(key_list[4], (D,), jnp.float32), 0.5, 1.5).astype(jnp.bfloat16)
    router_weight = noise(key_list[5], (D, EXPERTS), (D * 32) ** -0.5, 0.01953125)
    router_bias = jnp.clip(jax.random.uniform(key_list[6], (EXPERTS,), jnp.float32, -0.4, 0.4), -0.4, 0.4)
    routes_keys = jax.random.split(jax.random.fold_in(key_list[7], 1), ROWS // ROWS_DEV)
    routes_turns = jax.random.permutation(jax.random.fold_in(key_list[7], 3), ROWS // ROWS_DEV)
    routes = jax.vmap(lambda own, number: shared_out(jax.random.fold_in(key_list[7], 2), own, number, ROWS_DEV, EXPERTS, TOP, CAP, 2))(routes_keys, routes_turns).reshape((ROWS, TOP))
    gate_up_weight = noise(key_list[8], (2 * EXPERTS, D, 2, FF // 2), (D // 6) ** -0.5, 0.25, ((0, 16), (3, 2)))
    gate_up_bias = noise(key_list[9], (2 * EXPERTS, 2, FF // 2), 0.5, 3.0, ((0, 16), (2, 2)))
    down_weight = noise(key_list[10], (2 * EXPERTS, FF // 2, D), (FF * 4) ** -0.5, 0.0546875, ((0, 16), (1, 2)))
    down_bias = noise(key_list[11], (EXPERTS, D), 0.5, 3.0)
    next_gain = jnp.clip(1.0 + 0.1 * jax.random.normal(key_list[12], (D,), jnp.float32), 0.5, 1.5).astype(jnp.bfloat16)
    return dict(attn_ctx=attn_ctx, o_weight=o_weight, o_bias=o_bias, residual=residual, post_gain=post_gain, router_weight=router_weight, router_bias=router_bias, routes=routes, gate_up_weight=gate_up_weight, gate_up_bias=gate_up_bias, down_weight=down_weight, down_bias=down_bias, next_gain=next_gain)


def rms_norm(values, gain):
    scale = lax.rsqrt(lax.optimization_barrier(jnp.mean(values * values, axis=-1, keepdims=True)) + 1e-05)
    return values * scale * gain.astype(jnp.float32)

def reference(attn_ctx, o_weight, o_bias, residual, post_gain, router_weight, router_bias, routes, gate_up_weight, gate_up_bias, down_weight, down_bias, next_gain):
    proj = jnp.dot(attn_ctx, o_weight, preferred_element_type=jnp.float32)
    state = (residual.astype(jnp.float32) + proj + o_bias.astype(jnp.float32)).astype(jnp.bfloat16)
    normed = rms_norm(state.astype(jnp.float32), post_gain).astype(jnp.bfloat16)
    logits = jnp.dot(normed, router_weight, preferred_element_type=jnp.float32) + router_bias.astype(jnp.float32)
    picked = jnp.take_along_axis(logits, routes, axis=1)
    expo = jnp.exp(picked)
    weights = expo / lax.optimization_barrier(jnp.sum(expo, axis=1, keepdims=True))
    most_rows = N_REQ * N_TP * CAP
    half_width = FF // 2
    part_width = FF // (2 * N_TP)
    normed_f = normed.astype(jnp.float32)

    def one_expert(expert, total):
        hits = routes == expert
        row_weight = lax.optimization_barrier(jnp.sum(jnp.where(hits, weights, jnp.zeros_like(weights)), axis=1))
        hit_any = jnp.any(hits, axis=1)
        keys = jnp.where(hit_any, 0, 1).astype(jnp.int32)
        order = jnp.argsort(keys, stable=True)[:most_rows].astype(jnp.int32)
        rows = normed_f[order]
        start = (2 * expert).astype(jnp.int32)
        w_pair = lax.dynamic_slice_in_dim(gate_up_weight, start, 2, 0).astype(jnp.float32)
        b_pair = lax.dynamic_slice_in_dim(gate_up_bias, start, 2, 0).astype(jnp.float32)
        w_gate = jnp.transpose(w_pair[:, :, 0, :], (1, 0, 2)).reshape(D, FF)
        w_up = jnp.transpose(w_pair[:, :, 1, :], (1, 0, 2)).reshape(D, FF)
        gate = jnp.dot(rows, w_gate) + b_pair[:, 0, :].reshape(FF)
        upper = jnp.dot(rows, w_up) + b_pair[:, 1, :].reshape(FF)
        gate = jnp.minimum(gate, 7.0)
        upper = jnp.clip(upper, -7.0, 7.0)
        act = ((upper + 1.0) * gate * jax.nn.sigmoid(1.702 * gate)).astype(jnp.bfloat16)
        down_pair = lax.dynamic_slice_in_dim(down_weight, start, 2, 0).astype(jnp.float32)
        down_parts = down_pair.reshape(2 * N_TP, part_width, D)
        act_parts = act.astype(jnp.float32).reshape(most_rows, 2 * N_TP, part_width)
        parts = jnp.einsum('npf,pfd->pnd', act_parts, down_parts)
        parts = lax.optimization_barrier(parts.astype(jnp.bfloat16)).astype(jnp.float32)
        bias_row = lax.dynamic_slice_in_dim(down_bias, expert.astype(jnp.int32), 1, 0).astype(jnp.float32)
        expert_out = lax.optimization_barrier(jnp.sum(parts, axis=0)) + bias_row
        return total.at[order].add(expert_out * row_weight[order][:, None])
    mixed = lax.fori_loop(0, EXPERTS, one_expert, jnp.zeros((ROWS, D), jnp.float32))
    hidden_state = (state.astype(jnp.float32) + mixed).astype(jnp.bfloat16)
    normed_out = rms_norm(hidden_state.astype(jnp.float32), next_gain).astype(jnp.bfloat16)
    return (hidden_state, normed_out)
```

```python
import jax
import jax.numpy as jnp
from jax import lax
from jax.sharding import PartitionSpec as P


def rms_norm(values, gain):
    scale = lax.rsqrt(jnp.mean(values * values, axis=-1, keepdims=True) + 1e-05)
    return values * scale * gain.astype(jnp.float32)


def route_rows(state, route_ids, post_gain, router_weight, router_bias, experts):
    normed = rms_norm(state.astype(jnp.float32), post_gain).astype(jnp.bfloat16)
    logits = jnp.dot(normed, router_weight, preferred_element_type=jnp.float32) + router_bias
    onehot = (route_ids[:, :, None] == jnp.arange(experts, dtype=jnp.int32)[None, None, :]).astype(
        jnp.float32
    )
    picked = jnp.sum(onehot * logits[:, None, :], axis=2)
    expo = jnp.exp(picked)
    weights = expo / jnp.sum(expo, axis=1, keepdims=True)
    table = jnp.sum(onehot * weights[:, :, None], axis=1)
    return (normed, weights, table)


def slot_numbers(route_blocks, experts, capacity):
    onehot = (
        route_blocks[:, :, None] == jnp.arange(experts, dtype=jnp.int32)[None, None, :]
    ).astype(jnp.int32)
    ranks = jnp.cumsum(onehot, axis=1) - onehot
    slots = jnp.sum(ranks * onehot, axis=2)
    offsets = jnp.arange(route_blocks.shape[0], dtype=jnp.int32)[:, None] * capacity
    return slots + offsets


def place_rows(normed, targets, block, req_count, top_count):
    width = normed.shape[1]
    source = jnp.repeat(normed, top_count, axis=0)
    buffer = jnp.zeros((req_count * block, width), jnp.bfloat16)
    index = jnp.concatenate([targets, targets + block])
    buffer = buffer.at[index].set(jnp.concatenate([source, source], axis=0))
    return buffer.reshape(req_count, block, width)


def weigh_parts(flat, targets, block, weights, top_count):
    first = jnp.take(flat, targets, axis=0).astype(jnp.float32)
    second = jnp.take(flat, targets + block, axis=0).astype(jnp.float32)
    values = (first + second) * weights.reshape(-1)[:, None]
    return jnp.sum(values.reshape(-1, top_count, flat.shape[1]), axis=1)


def expert_apply(rows, gate_up_weight, gate_up_bias, down_weight):
    local_width = gate_up_weight.shape[3]
    weight_mat = gate_up_weight[0].reshape(gate_up_weight.shape[1], 2 * local_width)
    projected = jnp.dot(rows, weight_mat, preferred_element_type=jnp.float32)
    projected = projected + gate_up_bias[0].reshape(2 * local_width).astype(jnp.float32)
    gate = jnp.minimum(projected[:, :local_width], 7.0)
    upper = jnp.clip(projected[:, local_width:], -7.0, 7.0)
    act = ((upper + 1.0) * gate * jax.nn.sigmoid(1.702 * gate)).astype(jnp.bfloat16)
    return jnp.dot(act, down_weight[0], preferred_element_type=jnp.float32)


def dense_experts(normed, table, gate_up_weight, gate_up_bias, down_weight):
    width = normed.shape[1]
    expert = lax.axis_index("req") // 2
    high = table.astype(jnp.bfloat16)
    low = (table - high.astype(jnp.float32)).astype(jnp.bfloat16)
    packed = jnp.concatenate([normed, high, low], axis=1)
    gathered = lax.all_gather(packed, ("req", "tp"), axis=0, tiled=True)
    count = table.shape[1]
    pick = (jnp.arange(2 * count, dtype=jnp.int32) % count == expert).astype(jnp.float32)
    share = jnp.sum(gathered[:, width:].astype(jnp.float32) * pick[None, :], axis=1, keepdims=True)
    part = expert_apply(gathered[:, :width], gate_up_weight, gate_up_bias, down_weight) * share
    return lax.psum_scatter(
        part.astype(jnp.bfloat16), ("req", "tp"), scatter_dimension=0, tiled=True
    ).astype(jnp.float32)


def per_device(
    attn_ctx,
    o_weight,
    o_bias,
    residual,
    post_gain,
    router_weight,
    router_bias,
    routes,
    gate_up_weight,
    gate_up_bias,
    down_weight,
    down_bias,
    next_gain,
):
    req_count = lax.axis_size("req")
    tp_count = lax.axis_size("tp")
    width = o_weight.shape[1]
    tokens_here = attn_ctx.shape[0]
    own_rows = tokens_here // tp_count
    experts = req_count // 2
    top_count = routes.shape[1]
    capacity = min(own_rows, max(2, 2 * top_count * own_rows // experts))
    own_start = lax.axis_index("tp") * own_rows
    bias_vec = o_bias.astype(jnp.float32)
    summed = lax.psum_scatter(
        jnp.dot(attn_ctx, o_weight, preferred_element_type=jnp.float32).astype(jnp.bfloat16),
        "tp",
        scatter_dimension=0,
        tiled=True,
    ).astype(jnp.float32)
    state = (residual.astype(jnp.float32) + summed + bias_vec).astype(jnp.bfloat16)
    own_routes = lax.dynamic_slice_in_dim(routes, own_start, own_rows, 0)
    normed, weights, table = route_rows(
        state, own_routes, post_gain, router_weight, router_bias, experts
    )
    bias_terms = jnp.dot(table, down_bias.astype(jnp.float32), precision=lax.Precision.HIGHEST)
    if capacity == own_rows:
        mixed = dense_experts(
            normed, table, gate_up_weight, gate_up_bias, down_weight
        )
        hidden_state = (state.astype(jnp.float32) + mixed + bias_terms).astype(jnp.bfloat16)
        normed_out = rms_norm(hidden_state.astype(jnp.float32), next_gain).astype(jnp.bfloat16)
        return (hidden_state, normed_out)
    slots = slot_numbers(own_routes.reshape(1, own_rows * top_count), experts, capacity)
    targets = 2 * own_routes.reshape(-1) * capacity + slots.reshape(-1)
    outgoing = place_rows(normed, targets, capacity, req_count, top_count)
    incoming = lax.all_to_all(outgoing, "req", split_axis=0, concat_axis=0, tiled=True)
    gathered = lax.all_gather(incoming[None], "tp", axis=0, tiled=True).reshape(-1, width)
    sums = lax.psum_scatter(
        expert_apply(gathered, gate_up_weight, gate_up_bias, down_weight).astype(jnp.bfloat16),
        "tp",
        scatter_dimension=0,
        tiled=True,
    ).astype(jnp.float32)
    returned = lax.all_to_all(
        sums.reshape(req_count, capacity, width).astype(jnp.bfloat16),
        "req",
        split_axis=0,
        concat_axis=0,
        tiled=True,
    ).astype(jnp.float32)
    mixed = weigh_parts(returned.reshape(-1, width), targets, capacity, weights, top_count)
    hidden_state = (state.astype(jnp.float32) + mixed + bias_terms).astype(jnp.bfloat16)
    normed_out = rms_norm(hidden_state.astype(jnp.float32), next_gain).astype(jnp.bfloat16)
    return (hidden_state, normed_out)


def solution(mesh):
    return jax.shard_map(
        per_device,
        mesh=mesh,
        in_specs=(
            P("req", "tp"),
            P("tp", None),
            P(),
            P(("req", "tp"), None),
            P(),
            P(),
            P(),
            P("req", None),
            P("req", None, None, "tp"),
            P("req", None, "tp"),
            P("req", "tp", None),
            P(),
            P(),
        ),
        out_specs=(P(("req", "tp"), None), P(("req", "tp"), None)),
        check_vma=False,
    )
```

```python
import functools

import jax
import jax.numpy as jnp
from jax import lax
from jax.experimental import pallas as pl
from jax.experimental.pallas import tpu as pltpu
from jax.sharding import PartitionSpec as P


def rms_norm(values, gain):
    scale = lax.rsqrt(jnp.mean(values * values, axis=-1, keepdims=True) + 1e-05)
    return values * scale * gain.astype(jnp.float32)


def route_rows(state, route_ids, post_gain, router_weight, router_bias, experts):
    normed = rms_norm(state.astype(jnp.float32), post_gain).astype(jnp.bfloat16)
    logits = jnp.dot(normed, router_weight, preferred_element_type=jnp.float32) + router_bias
    onehot = (route_ids[:, :, None] == jnp.arange(experts, dtype=jnp.int32)[None, None, :]).astype(
        jnp.float32
    )
    picked = jnp.sum(onehot * logits[:, None, :], axis=2)
    expo = jnp.exp(picked)
    weights = expo / jnp.sum(expo, axis=1, keepdims=True)
    table = jnp.sum(onehot * weights[:, :, None], axis=1)
    return (normed, weights, table)


def slot_numbers(route_blocks, experts, capacity):
    onehot = (
        route_blocks[:, :, None] == jnp.arange(experts, dtype=jnp.int32)[None, None, :]
    ).astype(jnp.int32)
    ranks = jnp.cumsum(onehot, axis=1) - onehot
    slots = jnp.sum(ranks * onehot, axis=2)
    offsets = jnp.arange(route_blocks.shape[0], dtype=jnp.int32)[:, None] * capacity
    return slots + offsets


def place_rows(normed, targets, block, req_count, top_count):
    width = normed.shape[1]
    source = jnp.repeat(normed, top_count, axis=0)
    buffer = jnp.zeros((req_count * block, width), jnp.bfloat16)
    index = jnp.concatenate([targets, targets + block])
    buffer = buffer.at[index].set(jnp.concatenate([source, source], axis=0))
    return buffer.reshape(req_count, block, width)


def weigh_parts(flat, targets, block, weights, top_count):
    first = jnp.take(flat, targets, axis=0).astype(jnp.float32)
    second = jnp.take(flat, targets + block, axis=0).astype(jnp.float32)
    values = (first + second) * weights.reshape(-1)[:, None]
    return jnp.sum(values.reshape(-1, top_count, flat.shape[1]), axis=1)


def expert_apply(rows, gate_up_weight, gate_up_bias, down_weight):
    local_width = gate_up_weight.shape[3]
    weight_mat = gate_up_weight[0].reshape(gate_up_weight.shape[1], 2 * local_width)
    projected = jnp.dot(rows, weight_mat, preferred_element_type=jnp.float32)
    projected = projected + gate_up_bias[0].reshape(2 * local_width).astype(jnp.float32)
    gate = jnp.minimum(projected[:, :local_width], 7.0)
    upper = jnp.clip(projected[:, local_width:], -7.0, 7.0)
    act = ((upper + 1.0) * gate * jax.nn.sigmoid(1.702 * gate)).astype(jnp.bfloat16)
    return jnp.dot(act, down_weight[0], preferred_element_type=jnp.float32)


def top_bit(slot):
    return slot.bit_length() - 1


def by_hops(slots):
    return sorted(slots, key=lambda slot: (bin(slot).count("1"), slot))


def partner_of(axis, stride):
    here = lax.axis_index(axis)
    return here + stride * (1 - 2 * ((here // stride) % 2))


def tree_copies(orders, rows, first_bit, last_bit):
    half_rows = rows // 2
    listed = {}
    for bit in range(first_bit, last_bit):
        for slot in range(1 << bit):
            if orders[0][bit] == orders[1][bit]:
                listed[(bit, slot, None)] = (slot * rows, rows)
            else:
                for half in range(2):
                    listed[(bit, slot, half)] = (slot * rows + half * half_rows, half_rows)
    return listed


def exchange_kernel(
    orders,
    rows,
    width,
    experts,
    x_ref,
    gate_up_ref,
    bias_ref,
    down_ref,
    out_ref,
    gathered,
    partial,
    received,
    gate_up,
    down,
    act,
    weight_sems,
    gather_send,
    gather_recv,
    reduce_send,
    reduce_recv,
):
    bits = len(orders[0])
    slots = 1 << bits
    half_rows = rows // 2
    hidden = down.shape[0]
    chunk = slots // 4
    span = chunk * rows
    tail = width // 128 * 128
    expert = lax.axis_index("req") // 2

    loads = [
        pltpu.make_async_copy(gate_up_ref, gate_up, weight_sems.at[0]),
        pltpu.make_async_copy(down_ref, down, weight_sems.at[1]),
    ]
    for load in loads:
        load.start()
    barrier = pltpu.get_barrier_semaphore()
    for axis, stride in orders[0]:
        pl.semaphore_signal(
            barrier,
            inc=1,
            device_id={axis: partner_of(axis, stride)},
            device_id_type=pl.DeviceIdType.MESH,
        )
    gathered[0:rows, :] = x_ref[...]
    pl.semaphore_wait(barrier, bits)

    def remote(source, target, send_sem, recv_sem, link):
        axis, stride = link
        return pltpu.make_async_remote_copy(
            src_ref=source,
            dst_ref=target,
            send_sem=send_sem,
            recv_sem=recv_sem,
            device_id={axis: partner_of(axis, stride)},
            device_id_type=pl.DeviceIdType.MESH,
        )

    spread = {}
    for number, (key, (row, length)) in enumerate(tree_copies(orders, rows, 0, bits).items()):
        bit, slot, half = key
        spread[key] = remote(
            gathered.at[pl.ds(row, length), :],
            gathered.at[pl.ds(row + (rows << bit), length), :],
            gather_send.at[number],
            gather_recv.at[number],
            orders[half or 0][bit],
        )

    def forward(slot):
        for bit in range(top_bit(slot) + 1, bits):
            for half in (None, 0, 1):
                if (bit, slot, half) in spread:
                    spread[(bit, slot, half)].start()

    def arrive(slot):
        bit = top_bit(slot)
        for half in (None, 0, 1):
            key = (bit, slot - (1 << bit), half)
            if key in spread:
                spread[key].wait_recv()

    def compute(first):
        base = first * rows
        block = pl.ds(base, span)
        for start in range(0, hidden, 256):
            size = min(256, hidden - start)
            sides = []
            for side in range(2):
                sides.append(
                    lax.dot_general(
                        gathered[block, 0:width],
                        gate_up[pl.ds(side * hidden + start, size), :],
                        (((1,), (1,)), ((), ())),
                        preferred_element_type=jnp.float32,
                    )
                    + bias_ref[side : side + 1, start : start + size]
                )
            gate = jnp.minimum(sides[0], 7.0)
            upper = jnp.clip(sides[1], -7.0, 7.0)
            act[:, start : start + size] = (
                (upper + 1.0) * gate * jax.nn.sigmoid(1.702 * gate)
            ).astype(jnp.bfloat16)
        extra = gathered[block, tail:].astype(jnp.float32)
        lane = lax.broadcasted_iota(jnp.int32, extra.shape, 1) - (width - tail)
        mine = (lane == expert) | (lane == expert + experts)
        share = jnp.sum(jnp.where(mine, extra, 0.0), axis=1, keepdims=True)
        for start in range(0, width, 768):
            size = min(768, width - start)
            partial[block, start : start + size] = (
                jnp.dot(
                    act[...], down[:, start : start + size], preferred_element_type=jnp.float32
                )
                * share
            ).astype(jnp.bfloat16)

    fold = {}
    number = 0
    for first in (slots // 2, slots // 2 + chunk):
        block = pl.ds(first * rows, span)
        fold[("chunk", first)] = remote(
            partial.at[block, :],
            received.at[block, :],
            reduce_send.at[number],
            reduce_recv.at[number],
            orders[0][bits - 1],
        )
        number += 1
    for key, (row, length) in tree_copies(orders, rows, 0, bits - 1).items():
        bit, slot, half = key
        block = pl.ds(row + (rows << bit), length)
        fold[(slot + (1 << bit), half)] = remote(
            partial.at[block, :],
            received.at[block, :],
            reduce_send.at[number],
            reduce_recv.at[number],
            orders[half or 0][bit],
        )
        number += 1
    landed = set()

    def await_fold(slot, half):
        if slot >= slots // 2:
            key = ("chunk", slot // chunk * chunk)
        else:
            key = (slot, half) if (slot, half) in fold else (slot, None)
        if key not in landed:
            landed.add(key)
            fold[key].wait_recv()

    def reduce(slot):
        for half in range(2):
            first = slot * rows + half * half_rows
            total = partial[first : first + half_rows, :].astype(jnp.float32)
            for bit in reversed(range(top_bit(slot) + 1, bits)):
                child = slot + (1 << bit)
                await_fold(child, half)
                begin = child * rows + half * half_rows
                total = total + received[begin : begin + half_rows, :].astype(jnp.float32)
            if slot == 0:
                out_ref[half * half_rows : (half + 1) * half_rows, :] = total
            else:
                partial[first : first + half_rows, :] = total.astype(jnp.bfloat16)
                if (slot, half) in fold:
                    fold[(slot, half)].start()
        if slot and (slot, None) in fold:
            fold[(slot, None)].start()

    forward(0)
    for slot in by_hops(range(1, chunk)):
        arrive(slot)
        forward(slot)
    for load in loads:
        load.wait()
    compute(0)
    early = by_hops(range(chunk, 2 * chunk))
    for slot in early[: chunk // 2]:
        arrive(slot)
        forward(slot)
    for slot in range(2 * chunk, 3 * chunk):
        arrive(slot)
    compute(2 * chunk)
    fold[("chunk", 2 * chunk)].start()
    for slot in early[chunk // 2 :]:
        arrive(slot)
        forward(slot)
    for slot in range(3 * chunk, 4 * chunk):
        arrive(slot)
    compute(3 * chunk)
    fold[("chunk", 3 * chunk)].start()
    compute(chunk)
    for slot in reversed(early):
        reduce(slot)
    for slot in reversed(by_hops(range(0, chunk))):
        reduce(slot)
    for copy in spread.values():
        copy.wait_send()
    for copy in fold.values():
        copy.wait_send()


def tree_orders(req_count, tp_count):
    strides = []
    stride = 1
    while stride < req_count:
        strides.append(("req", stride))
        stride *= 2
    crosses = []
    stride = 1
    while stride < tp_count:
        crosses.append(("tp", stride))
        stride *= 2
    return (
        strides[2:] + strides[1:2] + crosses + strides[:1],
        strides[2:] + crosses + strides[1:2] + strides[:1],
    )


def dense_experts(normed, table, gate_up_weight, gate_up_bias, down_weight):
    rows, width = normed.shape
    experts = table.shape[1]
    orders = tree_orders(lax.axis_size("req"), lax.axis_size("tp"))
    bits = len(orders[0])
    hidden = down_weight.shape[1]
    padded = (width + 2 * experts + 127) // 128 * 128
    high = table.astype(jnp.bfloat16)
    low = (table - high.astype(jnp.float32)).astype(jnp.bfloat16)
    packed = jnp.concatenate(
        [normed, high, low, jnp.zeros((rows, padded - width - 2 * experts), jnp.bfloat16)], axis=1
    )
    gate_up = jnp.transpose(gate_up_weight[0], (1, 2, 0)).reshape(2 * hidden, width)
    bias = gate_up_bias[0].astype(jnp.float32)
    total_rows = rows << bits
    copies = len(tree_copies(orders, rows, 0, bits))
    folds = 2 + len(tree_copies(orders, rows, 0, bits - 1))
    vmem = pl.BlockSpec(memory_space=pltpu.VMEM)
    anywhere = pl.BlockSpec(memory_space=pl.ANY)
    return pl.pallas_call(
        functools.partial(exchange_kernel, orders, rows, width, experts),
        out_shape=jax.ShapeDtypeStruct((rows, width), jnp.float32),
        in_specs=[vmem, anywhere, vmem, anywhere],
        out_specs=vmem,
        scratch_shapes=[
            pltpu.VMEM((total_rows, padded), jnp.bfloat16),
            pltpu.VMEM((total_rows, width), jnp.bfloat16),
            pltpu.VMEM((total_rows, width), jnp.bfloat16),
            pltpu.VMEM((2 * hidden, width), jnp.bfloat16),
            pltpu.VMEM((hidden, width), jnp.bfloat16),
            pltpu.VMEM((total_rows // 4, hidden), jnp.bfloat16),
            pltpu.SemaphoreType.DMA((2,)),
            pltpu.SemaphoreType.DMA((copies,)),
            pltpu.SemaphoreType.DMA((copies,)),
            pltpu.SemaphoreType.DMA((folds,)),
            pltpu.SemaphoreType.DMA((folds,)),
        ],
        compiler_params=pltpu.CompilerParams(
            collective_id=0, has_side_effects=True, vmem_limit_bytes=56 * 1024 * 1024
        ),
    )(packed, gate_up, bias, down_weight[0])


def tree_fits(req_count, tp_count, rows):
    count = req_count * tp_count
    return count >= 16 and req_count >= 8 and tp_count >= 2 and count & (count - 1) == 0 and rows % 32 == 0


def per_device(
    attn_ctx,
    o_weight,
    o_bias,
    residual,
    post_gain,
    router_weight,
    router_bias,
    routes,
    gate_up_weight,
    gate_up_bias,
    down_weight,
    down_bias,
    next_gain,
):
    req_count = lax.axis_size("req")
    tp_count = lax.axis_size("tp")
    width = o_weight.shape[1]
    tokens_here = attn_ctx.shape[0]
    own_rows = tokens_here // tp_count
    experts = req_count // 2
    top_count = routes.shape[1]
    capacity = min(own_rows, max(2, 2 * top_count * own_rows // experts))
    own_start = lax.axis_index("tp") * own_rows
    bias_vec = o_bias.astype(jnp.float32)
    summed = lax.psum_scatter(
        jnp.dot(attn_ctx, o_weight, preferred_element_type=jnp.float32).astype(jnp.bfloat16),
        "tp",
        scatter_dimension=0,
        tiled=True,
    ).astype(jnp.float32)
    state = (residual.astype(jnp.float32) + summed + bias_vec).astype(jnp.bfloat16)
    own_routes = lax.dynamic_slice_in_dim(routes, own_start, own_rows, 0)
    normed, weights, table = route_rows(
        state, own_routes, post_gain, router_weight, router_bias, experts
    )
    bias_terms = jnp.dot(table, down_bias.astype(jnp.float32), precision=lax.Precision.HIGHEST)
    if capacity == own_rows and tree_fits(req_count, tp_count, own_rows):
        mixed = dense_experts(
            normed, table, gate_up_weight, gate_up_bias, down_weight
        )
        hidden_state = (state.astype(jnp.float32) + mixed + bias_terms).astype(jnp.bfloat16)
        normed_out = rms_norm(hidden_state.astype(jnp.float32), next_gain).astype(jnp.bfloat16)
        return (hidden_state, normed_out)
    slots = slot_numbers(own_routes.reshape(1, own_rows * top_count), experts, capacity)
    targets = 2 * own_routes.reshape(-1) * capacity + slots.reshape(-1)
    outgoing = place_rows(normed, targets, capacity, req_count, top_count)
    incoming = lax.all_to_all(outgoing, "req", split_axis=0, concat_axis=0, tiled=True)
    gathered = lax.all_gather(incoming[None], "tp", axis=0, tiled=True).reshape(-1, width)
    sums = lax.psum_scatter(
        expert_apply(gathered, gate_up_weight, gate_up_bias, down_weight).astype(jnp.bfloat16),
        "tp",
        scatter_dimension=0,
        tiled=True,
    ).astype(jnp.float32)
    returned = lax.all_to_all(
        sums.reshape(req_count, capacity, width).astype(jnp.bfloat16),
        "req",
        split_axis=0,
        concat_axis=0,
        tiled=True,
    ).astype(jnp.float32)
    mixed = weigh_parts(returned.reshape(-1, width), targets, capacity, weights, top_count)
    hidden_state = (state.astype(jnp.float32) + mixed + bias_terms).astype(jnp.bfloat16)
    normed_out = rms_norm(hidden_state.astype(jnp.float32), next_gain).astype(jnp.bfloat16)
    return (hidden_state, normed_out)


def solution(mesh):
    return jax.shard_map(
        per_device,
        mesh=mesh,
        in_specs=(
            P("req", "tp"),
            P("tp", None),
            P(),
            P(("req", "tp"), None),
            P(),
            P(),
            P(),
            P("req", None),
            P("req", None, None, "tp"),
            P("req", None, "tp"),
            P("req", "tp", None),
            P(),
            P(),
        ),
        out_specs=(P(("req", "tp"), None), P(("req", "tp"), None)),
        check_vma=False,
    )
```

```python
import functools

import jax
import jax.numpy as jnp
from jax import lax
from jax.experimental import pallas as pl
from jax.experimental.pallas import tpu as pltpu
from jax.sharding import PartitionSpec as P


def rms_norm(values, gain):
    scale = lax.rsqrt(jnp.mean(values * values, axis=-1, keepdims=True) + 1e-05)
    return values * scale * gain.astype(jnp.float32)


def route_rows(state, route_ids, post_gain, router_weight, router_bias, experts):
    normed = rms_norm(state.astype(jnp.float32), post_gain).astype(jnp.bfloat16)
    logits = jnp.dot(normed, router_weight, preferred_element_type=jnp.float32) + router_bias
    onehot = (route_ids[:, :, None] == jnp.arange(experts, dtype=jnp.int32)[None, None, :]).astype(
        jnp.float32
    )
    picked = jnp.sum(onehot * logits[:, None, :], axis=2)
    expo = jnp.exp(picked)
    weights = expo / jnp.sum(expo, axis=1, keepdims=True)
    table = jnp.sum(onehot * weights[:, :, None], axis=1)
    return (normed, weights, table)


def slot_numbers(route_blocks, experts, capacity):
    onehot = (
        route_blocks[:, :, None] == jnp.arange(experts, dtype=jnp.int32)[None, None, :]
    ).astype(jnp.int32)
    ranks = jnp.cumsum(onehot, axis=1) - onehot
    slots = jnp.sum(ranks * onehot, axis=2)
    offsets = jnp.arange(route_blocks.shape[0], dtype=jnp.int32)[:, None] * capacity
    return slots + offsets


def place_rows(normed, targets, block, req_count, top_count):
    width = normed.shape[1]
    source = jnp.repeat(normed, top_count, axis=0)
    buffer = jnp.zeros((req_count * block, width), jnp.bfloat16)
    index = jnp.concatenate([targets, targets + block])
    buffer = buffer.at[index].set(jnp.concatenate([source, source], axis=0))
    return buffer.reshape(req_count, block, width)


def weigh_parts(flat, targets, block, weights, top_count):
    first = jnp.take(flat, targets, axis=0).astype(jnp.float32)
    second = jnp.take(flat, targets + block, axis=0).astype(jnp.float32)
    values = (first + second) * weights.reshape(-1)[:, None]
    return jnp.sum(values.reshape(-1, top_count, flat.shape[1]), axis=1)


def expert_apply(rows, gate_up_weight, gate_up_bias, down_weight):
    local_width = gate_up_weight.shape[3]
    weight_mat = gate_up_weight[0].reshape(gate_up_weight.shape[1], 2 * local_width)
    projected = jnp.dot(rows, weight_mat, preferred_element_type=jnp.float32)
    projected = projected + gate_up_bias[0].reshape(2 * local_width).astype(jnp.float32)
    gate = jnp.minimum(projected[:, :local_width], 7.0)
    upper = jnp.clip(projected[:, local_width:], -7.0, 7.0)
    act = ((upper + 1.0) * gate * jax.nn.sigmoid(1.702 * gate)).astype(jnp.bfloat16)
    return jnp.dot(act, down_weight[0], preferred_element_type=jnp.float32)


def top_bit(slot):
    return slot.bit_length() - 1


def by_hops(slots):
    return sorted(slots, key=lambda slot: (bin(slot).count("1"), slot))


def partner_of(axis, stride):
    here = lax.axis_index(axis)
    return here + stride * (1 - 2 * ((here // stride) % 2))


def tree_copies(orders, rows, first_bit, last_bit):
    half_rows = rows // 2
    listed = {}
    for bit in range(first_bit, last_bit):
        for slot in range(1 << bit):
            if orders[0][bit] == orders[1][bit]:
                listed[(bit, slot, None)] = (slot * rows, rows)
            else:
                for half in range(2):
                    listed[(bit, slot, half)] = (slot * rows + half * half_rows, half_rows)
    return listed


def exchange_kernel(
    orders,
    rows,
    width,
    experts,
    x_ref,
    gate_up_ref,
    bias_ref,
    down_ref,
    out_ref,
    gathered,
    partial,
    received,
    gate_up,
    down,
    act,
    weight_sems,
    gather_send,
    gather_recv,
    reduce_send,
    reduce_recv,
):
    bits = len(orders[0])
    slots = 1 << bits
    half_rows = rows // 2
    hidden = down.shape[0]
    chunk = slots // 4
    span = chunk * rows
    tail = width // 128 * 128
    expert = lax.axis_index("req") // 2

    loads = [
        pltpu.make_async_copy(gate_up_ref, gate_up, weight_sems.at[0]),
        pltpu.make_async_copy(down_ref, down, weight_sems.at[1]),
    ]
    for load in loads:
        load.start()
    barrier = pltpu.get_barrier_semaphore()
    for axis, stride in orders[0]:
        pl.semaphore_signal(
            barrier,
            inc=1,
            device_id={axis: partner_of(axis, stride)},
            device_id_type=pl.DeviceIdType.MESH,
        )
    gathered[0:rows, :] = x_ref[...]
    pl.semaphore_wait(barrier, bits)

    def remote(source, target, send_sem, recv_sem, link):
        axis, stride = link
        return pltpu.make_async_remote_copy(
            src_ref=source,
            dst_ref=target,
            send_sem=send_sem,
            recv_sem=recv_sem,
            device_id={axis: partner_of(axis, stride)},
            device_id_type=pl.DeviceIdType.MESH,
        )

    spread = {}
    for number, (key, (row, length)) in enumerate(tree_copies(orders, rows, 0, bits).items()):
        bit, slot, half = key
        spread[key] = remote(
            gathered.at[pl.ds(row, length), :],
            gathered.at[pl.ds(row + (rows << bit), length), :],
            gather_send.at[number],
            gather_recv.at[number],
            orders[half or 0][bit],
        )

    def forward(slot):
        for bit in range(top_bit(slot) + 1, bits):
            for half in (None, 0, 1):
                if (bit, slot, half) in spread:
                    spread[(bit, slot, half)].start()

    def arrive(slot):
        bit = top_bit(slot)
        for half in (None, 0, 1):
            key = (bit, slot - (1 << bit), half)
            if key in spread:
                spread[key].wait_recv()

    def compute(first):
        base = first * rows
        block = pl.ds(base, span)
        for start in range(0, hidden, 256):
            size = min(256, hidden - start)
            sides = []
            for side in range(2):
                sides.append(
                    lax.dot_general(
                        gathered[block, 0:width],
                        gate_up[pl.ds(side * hidden + start, size), :],
                        (((1,), (1,)), ((), ())),
                        preferred_element_type=jnp.float32,
                    )
                    + bias_ref[side : side + 1, start : start + size]
                )
            gate = jnp.minimum(sides[0], 7.0)
            upper = jnp.clip(sides[1], -7.0, 7.0)
            act[:, start : start + size] = (
                (upper + 1.0) * gate * jax.nn.sigmoid(1.702 * gate)
            ).astype(jnp.bfloat16)
        extra = gathered[block, tail:].astype(jnp.float32)
        lane = lax.broadcasted_iota(jnp.int32, extra.shape, 1) - (width - tail)
        mine = (lane == expert) | (lane == expert + experts)
        share = jnp.sum(jnp.where(mine, extra, 0.0), axis=1, keepdims=True)
        for start in range(0, width, 768):
            size = min(768, width - start)
            partial[block, start : start + size] = (
                jnp.dot(
                    act[...], down[:, start : start + size], preferred_element_type=jnp.float32
                )
                * share
            ).astype(jnp.bfloat16)

    fold = {}
    number = 0
    for first in (slots // 2, slots // 2 + chunk):
        block = pl.ds(first * rows, span)
        fold[("chunk", first)] = remote(
            partial.at[block, :],
            received.at[block, :],
            reduce_send.at[number],
            reduce_recv.at[number],
            orders[0][bits - 1],
        )
        number += 1
    for key, (row, length) in tree_copies(orders, rows, 0, bits - 1).items():
        bit, slot, half = key
        block = pl.ds(row + (rows << bit), length)
        fold[(slot + (1 << bit), half)] = remote(
            partial.at[block, :],
            received.at[block, :],
            reduce_send.at[number],
            reduce_recv.at[number],
            orders[half or 0][bit],
        )
        number += 1
    landed = set()

    def await_fold(slot, half):
        if slot >= slots // 2:
            key = ("chunk", slot // chunk * chunk)
        else:
            key = (slot, half) if (slot, half) in fold else (slot, None)
        if key not in landed:
            landed.add(key)
            fold[key].wait_recv()

    def reduce(slot):
        for half in range(2):
            first = slot * rows + half * half_rows
            total = partial[first : first + half_rows, :].astype(jnp.float32)
            for bit in reversed(range(top_bit(slot) + 1, bits)):
                child = slot + (1 << bit)
                await_fold(child, half)
                begin = child * rows + half * half_rows
                total = total + received[begin : begin + half_rows, :].astype(jnp.float32)
            if slot == 0:
                out_ref[half * half_rows : (half + 1) * half_rows, :] = total
            else:
                partial[first : first + half_rows, :] = total.astype(jnp.bfloat16)
                if (slot, half) in fold:
                    fold[(slot, half)].start()
        if slot and (slot, None) in fold:
            fold[(slot, None)].start()

    forward(0)
    for slot in by_hops(range(1, chunk)):
        arrive(slot)
        forward(slot)
    for load in loads:
        load.wait()
    compute(0)
    early = by_hops(range(chunk, 2 * chunk))
    for slot in early[: chunk // 2]:
        arrive(slot)
        forward(slot)
    for slot in range(2 * chunk, 3 * chunk):
        arrive(slot)
    compute(2 * chunk)
    fold[("chunk", 2 * chunk)].start()
    for slot in early[chunk // 2 :]:
        arrive(slot)
        forward(slot)
    for slot in range(3 * chunk, 4 * chunk):
        arrive(slot)
    compute(3 * chunk)
    fold[("chunk", 3 * chunk)].start()
    compute(chunk)
    for slot in reversed(early):
        reduce(slot)
    for slot in reversed(by_hops(range(0, chunk))):
        reduce(slot)
    for copy in spread.values():
        copy.wait_send()
    for copy in fold.values():
        copy.wait_send()


def tree_orders(req_count, tp_count):
    strides = []
    stride = 1
    while stride < req_count:
        strides.append(("req", stride))
        stride *= 2
    crosses = []
    stride = 1
    while stride < tp_count:
        crosses.append(("tp", stride))
        stride *= 2
    return (
        strides[2:] + strides[1:2] + crosses + strides[:1],
        strides[2:] + crosses + strides[1:2] + strides[:1],
    )


def dense_experts(normed, table, gate_up_weight, gate_up_bias, down_weight):
    rows, width = normed.shape
    experts = table.shape[1]
    orders = tree_orders(lax.axis_size("req"), lax.axis_size("tp"))
    bits = len(orders[0])
    hidden = down_weight.shape[1]
    padded = (width + 2 * experts + 127) // 128 * 128
    high = table.astype(jnp.bfloat16)
    low = (table - high.astype(jnp.float32)).astype(jnp.bfloat16)
    packed = jnp.concatenate(
        [normed, high, low, jnp.zeros((rows, padded - width - 2 * experts), jnp.bfloat16)], axis=1
    )
    gate_up = jnp.transpose(gate_up_weight[0], (1, 2, 0)).reshape(2 * hidden, width)
    bias = gate_up_bias[0].astype(jnp.float32)
    total_rows = rows << bits
    copies = len(tree_copies(orders, rows, 0, bits))
    folds = 2 + len(tree_copies(orders, rows, 0, bits - 1))
    vmem = pl.BlockSpec(memory_space=pltpu.VMEM)
    anywhere = pl.BlockSpec(memory_space=pl.ANY)
    return pl.pallas_call(
        functools.partial(exchange_kernel, orders, rows, width, experts),
        out_shape=jax.ShapeDtypeStruct((rows, width), jnp.float32),
        in_specs=[vmem, anywhere, vmem, anywhere],
        out_specs=vmem,
        scratch_shapes=[
            pltpu.VMEM((total_rows, padded), jnp.bfloat16),
            pltpu.VMEM((total_rows, width), jnp.bfloat16),
            pltpu.VMEM((total_rows, width), jnp.bfloat16),
            pltpu.VMEM((2 * hidden, width), jnp.bfloat16),
            pltpu.VMEM((hidden, width), jnp.bfloat16),
            pltpu.VMEM((total_rows // 4, hidden), jnp.bfloat16),
            pltpu.SemaphoreType.DMA((2,)),
            pltpu.SemaphoreType.DMA((copies,)),
            pltpu.SemaphoreType.DMA((copies,)),
            pltpu.SemaphoreType.DMA((folds,)),
            pltpu.SemaphoreType.DMA((folds,)),
        ],
        compiler_params=pltpu.CompilerParams(
            collective_id=0, has_side_effects=True, vmem_limit_bytes=56 * 1024 * 1024
        ),
    )(packed, gate_up, bias, down_weight[0])


def tree_fits(req_count, tp_count, rows):
    count = req_count * tp_count
    return count >= 16 and req_count >= 8 and tp_count >= 2 and count & (count - 1) == 0 and rows % 32 == 0


def per_device(
    attn_ctx,
    o_weight,
    o_bias,
    residual,
    post_gain,
    router_weight,
    router_bias,
    routes,
    gate_up_weight,
    gate_up_bias,
    down_weight,
    down_bias,
    next_gain,
):
    req_count = lax.axis_size("req")
    tp_count = lax.axis_size("tp")
    width = o_weight.shape[1]
    tokens_here = attn_ctx.shape[0]
    own_rows = tokens_here // tp_count
    experts = req_count // 2
    top_count = routes.shape[1]
    capacity = min(own_rows, max(2, 2 * top_count * own_rows // experts))
    own_start = lax.axis_index("tp") * own_rows
    bias_vec = o_bias.astype(jnp.float32)
    proj = jnp.dot(attn_ctx, o_weight, preferred_element_type=jnp.float32).astype(jnp.bfloat16)
    if tp_count == 2:
        theirs = lax.dynamic_slice_in_dim(proj, own_rows - own_start, own_rows, 0)
        mine = lax.dynamic_slice_in_dim(proj, own_start, own_rows, 0)
        arrived = lax.ppermute(theirs, "tp", [(0, 1), (1, 0)])
        summed = mine.astype(jnp.float32) + arrived.astype(jnp.float32)
    else:
        summed = lax.psum_scatter(proj, "tp", scatter_dimension=0, tiled=True).astype(jnp.float32)
    state = (residual.astype(jnp.float32) + summed + bias_vec).astype(jnp.bfloat16)
    own_routes = lax.dynamic_slice_in_dim(routes, own_start, own_rows, 0)
    normed, weights, table = route_rows(
        state, own_routes, post_gain, router_weight, router_bias, experts
    )
    bias_terms = jnp.dot(table, down_bias.astype(jnp.float32), precision=lax.Precision.HIGHEST)
    if capacity == own_rows and tree_fits(req_count, tp_count, own_rows):
        mixed = dense_experts(
            normed, table, gate_up_weight, gate_up_bias, down_weight
        )
        hidden_state = (state.astype(jnp.float32) + mixed + bias_terms).astype(jnp.bfloat16)
        normed_out = rms_norm(hidden_state.astype(jnp.float32), next_gain).astype(jnp.bfloat16)
        return (hidden_state, normed_out)
    slots = slot_numbers(own_routes.reshape(1, own_rows * top_count), experts, capacity)
    targets = 2 * own_routes.reshape(-1) * capacity + slots.reshape(-1)
    outgoing = place_rows(normed, targets, capacity, req_count, top_count)
    incoming = lax.all_to_all(outgoing, "req", split_axis=0, concat_axis=0, tiled=True)
    gathered = lax.all_gather(incoming[None], "tp", axis=0, tiled=True).reshape(-1, width)
    sums = lax.psum_scatter(
        expert_apply(gathered, gate_up_weight, gate_up_bias, down_weight).astype(jnp.bfloat16),
        "tp",
        scatter_dimension=0,
        tiled=True,
    ).astype(jnp.float32)
    returned = lax.all_to_all(
        sums.reshape(req_count, capacity, width).astype(jnp.bfloat16),
        "req",
        split_axis=0,
        concat_axis=0,
        tiled=True,
    ).astype(jnp.float32)
    mixed = weigh_parts(returned.reshape(-1, width), targets, capacity, weights, top_count)
    hidden_state = (state.astype(jnp.float32) + mixed + bias_terms).astype(jnp.bfloat16)
    normed_out = rms_norm(hidden_state.astype(jnp.float32), next_gain).astype(jnp.bfloat16)
    return (hidden_state, normed_out)


def solution(mesh):
    return jax.shard_map(
        per_device,
        mesh=mesh,
        in_specs=(
            P("req", "tp"),
            P("tp", None),
            P(),
            P(("req", "tp"), None),
            P(),
            P(),
            P(),
            P("req", None),
            P("req", None, None, "tp"),
            P("req", None, "tp"),
            P("req", "tp", None),
            P(),
            P(),
        ),
        out_specs=(P(("req", "tp"), None), P(("req", "tp"), None)),
        check_vma=False,
    )
```
